32 devices in a mesh: dp: 4 (over z), ctx: 8 (over y, x, core).
Axes of the slice: x: 2, y: 2, z: 4, core: 2. Of those that a mesh axis runs over, the one named last changes fastest.
Arguments:
- queries: bfloat16 [8192, 4096], P(('dp', 'ctx')), parts along dimension 0, may hold values from -24 to 24
- keys: bfloat16 [8192, 4096], P(('dp', 'ctx')), parts along dimension 0, may hold values from -24 to 24
- values: bfloat16 [8192, 4096], P(('dp', 'ctx')), parts along dimension 0, may hold values from -12 to 12
- mem_keys: bfloat16 [64, 512, 4096], P(('dp', 'ctx')), parts along dimension 0, may hold values from -9 to 9
- mem_values: bfloat16 [64, 512, 4096], P(('dp', 'ctx')), parts along dimension 0, may hold values from -12 to 12
- mem_ids: int32 [128, 2, 2], P('dp'), parts along dimension 0, may hold values from 0 to 15, as said below
Outputs:
- attended: bfloat16 [8192, 4096], P(('dp', 'ctx')), parts along dimension 0
The draws below stay inside these ranges and needn't reach their ends.
There are 4 independent parts, one for each index of `dp`. The reference program is written for one: setup_inputs(seed, part) draws one part's arguments, and reference() takes and returns one part's arrays. A program takes and returns all parts, laid end to end along the dimension named above; each array names one. Nothing has to cross between parts.
Inputs may be any that keep to these rules, and one draw needn't show every extreme that they name: mem_ids[h, t, :] names 2 memory blocks (one block may be named twice). Among the lists of each aligned group of 4 heads, at most 4 entries name blocks of one holder (blocks k * 2 to k * 2 + 1), and in every draw the blocks of some holder are named exactly 4 times by every group.
All inputs are finite; a program needn't handle non-finite values.
Results may differ from the reference program's by a relative error of at most 0.0045.
Values may be sent and summed in bfloat16 or wider, within the bound.
A program may use at most 192 MiB of HBM per device.

```python
import jax
import jax.numpy as jnp
from jax import lax

H = 32
HD = 128
TOK_DEV = 256
QT = 1024
MEM_BLK = 512
MTOP = 2
NBLK_DEV = 2
TOKENS = 2048
TILES = 2
NBLK = 16
N_CTX = 8


def paired_draw(key):
    base_key = jax.random.fold_in(key, 7)
    query_key, key_key = jax.random.split(base_key, 2)
    query_rows = 1.5 * jax.random.normal(query_key, (TOKENS, H * HD), jnp.float32)
    key_rows = 1.5 * jax.random.normal(key_key, (TOKENS, H * HD), jnp.float32)
    return (jnp.clip(query_rows, -24.0, 24.0), jnp.clip(key_rows, -24.0, 24.0))


def draw_queries(key, part):
    return paired_draw(key)[0].astype(jnp.bfloat16)


def draw_keys(key, part):
    return paired_draw(key)[1].astype(jnp.bfloat16)


def draw_mem_ids(key, part):
    requests = H * TOK_DEV * MTOP // QT
    capacity = max(2, 2 * requests // N_CTX)
    base_key = jax.random.fold_in(key, 23)
    star_key, ranking_key, local_key = jax.random.split(base_key, 3)
    popular = jax.random.randint(star_key, (), 0, N_CTX)
    pool_owner = jnp.arange(N_CTX * capacity, dtype=jnp.int32) % N_CTX

    def one_device(device_key):
        first_key, second_key = jax.random.split(device_key)
        ranking = jax.random.permutation(first_key, N_CTX * capacity).astype(jnp.int32)
        priority = jnp.where(pool_owner == popular, -1, ranking)
        chosen = jnp.argsort(priority, stable=True)[:requests]
        owners = pool_owner[chosen]
        return owners[jax.random.permutation(second_key, requests)]
    owners = jax.vmap(one_device)(jax.random.split(ranking_key, N_CTX))
    local_block = jax.random.randint(local_key, (N_CTX, requests), 0, NBLK_DEV)
    block_ids = owners * NBLK_DEV + local_block
    return block_ids.reshape(H, TOKENS // QT, MTOP).astype(jnp.int32)


def block_levels(key, shape, cuts, smallest, high):
    gain = 1.0
    for position, parts in cuts:
        heights = jax.random.uniform(jax.random.fold_in(jax.random.fold_in(key, 6), position), (parts,), jnp.float32, smallest / len(cuts), high / len(cuts))
        gain = gain * jnp.repeat(jnp.exp(heights), shape[position] // parts).reshape((-1,) + (1,) * (len(shape) - 1 - position))
    return gain


def centred(rng, dims, width, limit, cuts=(), kind=jnp.bfloat16):
    entries = jax.random.normal(rng, dims, jnp.float32) * width
    if len(cuts) > 0:
        entries = block_levels(rng, dims, cuts, -0.22, 0.18) * entries
    return jnp.clip(entries, min=-limit, max=limit).astype(kind)


def setup_inputs(seed: int = 0, part: int = 0) -> dict:
    streams_of = jax.random.split(jax.random.key(seed), 7)
    part_splits = jax.random.split(jax.random.fold_in(streams_of[6], part), 7)
    queries = draw_queries(jax.random.fold_in(jax.random.fold_in(streams_of[6], part), 71), part)
    keys = draw_keys(jax.random.fold_in(jax.random.fold_in(streams_of[6], part), 71), part)
    values = centred(part_splits[2], (TOKENS, H * HD), 2.0, 12.0, ((0, 8),))
    mem_keys = centred(part_splits[3], (NBLK, MEM_BLK, H * HD), 1.5, 9.0, ((0, 8),))
    mem_values = centred(part_splits[4], (NBLK, MEM_BLK, H * HD), 2.0, 12.0, ((0, 8),))
    mem_ids = draw_mem_ids(jax.random.fold_in(jax.random.fold_in(streams_of[6], part), 71), part)
    return {"queries": queries, "keys": keys, "values": values, "mem_keys": mem_keys, "mem_values": mem_values, "mem_ids": mem_ids}


def head_output(query_head, key_head, value_head, listed_keys, listed_values):
    inverse_root = HD ** -0.5
    query_wide = query_head.astype(jnp.float32)
    local_scores = jnp.dot(query_wide, key_head.astype(jnp.float32).T) * inverse_root
    positions = jnp.arange(TOKENS, dtype=jnp.int32)
    visible = positions[:, None] >= positions[None, :]
    local_scores = jnp.where(visible, local_scores, -jnp.inf)
    tiled_queries = query_wide.reshape(TILES, QT, HD)
    memory_scores = jnp.einsum("tqd,tkd->tqk", tiled_queries, listed_keys.astype(jnp.float32)) * inverse_root
    memory_scores = memory_scores.reshape(TOKENS, MTOP * MEM_BLK)
    row_max = jnp.maximum(jnp.max(local_scores, axis=1), jnp.max(memory_scores, axis=1))
    local_weights = jnp.exp(local_scores - row_max[:, None])
    memory_weights = jnp.exp(memory_scores - row_max[:, None])
    weight_sum = jnp.sum(local_weights, axis=1) + jnp.sum(memory_weights, axis=1)
    local_rounded = lax.optimization_barrier(local_weights.astype(jnp.bfloat16)).astype(jnp.float32)
    memory_rounded = lax.optimization_barrier(memory_weights.astype(jnp.bfloat16)).astype(jnp.float32)
    numerator = jnp.dot(local_rounded, value_head.astype(jnp.float32))
    memory_part = jnp.einsum("tqk,tkd->tqd", memory_rounded.reshape(TILES, QT, MTOP * MEM_BLK), listed_values.astype(jnp.float32))
    numerator = numerator + memory_part.reshape(TOKENS, HD)
    return numerator / weight_sum[:, None]


def reference(queries, keys, values, mem_keys, mem_values, mem_ids):
    def per_head(head):
        query_head = lax.dynamic_slice_in_dim(queries, head * HD, HD, 1)
        key_head = lax.dynamic_slice_in_dim(keys, head * HD, HD, 1)
        value_head = lax.dynamic_slice_in_dim(values, head * HD, HD, 1)
        head_ids = lax.dynamic_index_in_dim(mem_ids, head, 0, keepdims=False).reshape(-1).astype(jnp.int32)
        key_columns = lax.dynamic_slice_in_dim(mem_keys, head * HD, HD, 2)
        value_columns = lax.dynamic_slice_in_dim(mem_values, head * HD, HD, 2)
        listed_keys = jnp.take(key_columns, head_ids, axis=0).reshape(TILES, MTOP * MEM_BLK, HD)
        listed_values = jnp.take(value_columns, head_ids, axis=0).reshape(TILES, MTOP * MEM_BLK, HD)
        return head_output(query_head, key_head, value_head, listed_keys, listed_values)

    outputs = lax.map(per_head, jnp.arange(H, dtype=jnp.int32))
    return outputs.transpose(1, 0, 2).reshape(TOKENS, H * HD).astype(jnp.bfloat16)
```

```python
import functools
import math

import jax
import jax.numpy as jnp
from jax import lax
from jax.experimental import pallas as pl
from jax.experimental.pallas import tpu as pltpu
from jax.sharding import PartitionSpec as P

HD = 128
CHUNK = 512
MESH = pl.DeviceIdType.MESH


def entry_tables(mem_ids, devices, device_index, blocks_here, capacity):
    head_count, tile_count, listed = mem_ids.shape
    entries = head_count * tile_count * listed // devices
    per_head = tile_count * listed
    heads_here = head_count // devices
    ids = mem_ids.reshape(devices, entries)
    holder = ids // blocks_here
    position = jnp.arange(entries, dtype=jnp.int32)
    same = holder[:, :, None] == holder[:, None, :]
    earlier = position[None, :] < position[:, None]
    rank = jnp.sum((same & earlier[None]).astype(jnp.int32), axis=2)
    slots = jnp.arange(capacity, dtype=jnp.int32)
    chosen = (holder[:, None, :] == device_index) & (rank[:, None, :] == slots[None, :, None])
    head = jnp.arange(devices, dtype=jnp.int32)[:, None] * heads_here + position[None, :] // per_head
    code = head * blocks_here + ids % blocks_here
    send_table = jnp.sum(jnp.where(chosen, code[:, None, :], 0), axis=2).reshape(-1)
    own = jnp.arange(devices, dtype=jnp.int32)[:, None] == device_index
    receive_table = jnp.sum(jnp.where(own, holder * capacity + rank, 0), axis=0)
    return send_table, receive_table


def kernel(
    devices, capacity, tile_count, listed,
    send_table, receive_table, q_hbm, k_hbm, v_hbm, mk_hbm, mv_hbm, out_hbm,
    q_in, k_in, v_in, store_k, store_v, packed, arrived, out_buf,
    qkv_recv, qkv_send, mem_load, mem_recv, mem_send, out_recv, out_send,
):
    me = lax.axis_index("ctx")
    heads_here, span, _ = q_in.shape
    rows = q_hbm.shape[0]
    blocks_here, block_rows, columns = mk_hbm.shape
    head_count = columns // HD
    tile_rows = span // tile_count
    chunks = span // CHUNK
    peers_per_chunk = CHUNK // rows
    pieces = capacity * 2
    exponent_scale = HD ** (-0.5) * math.log2(math.e)

    def columns_of(head):
        return pl.ds(pl.multiple_of(head * HD, HD), HD)

    def rows_of(device):
        return pl.ds(pl.multiple_of(device * rows, rows), rows)

    def load_head(head, carry):
        for source, target, which in ((mk_hbm, store_k, 0), (mv_hbm, store_v, 1)):
            pltpu.make_async_copy(
                source.at[:, :, columns_of(head)],
                target.at[pl.ds(head * blocks_here, blocks_here)],
                mem_load.at[which],
            ).start()
        return carry

    lax.fori_loop(0, head_count, load_head, 0)

    barrier = pltpu.get_barrier_semaphore()

    def greet(offset, carry):
        pl.semaphore_signal(
            barrier, inc=1, device_id={"ctx": lax.rem(me + offset, devices)}, device_id_type=MESH
        )
        return carry

    lax.fori_loop(1, devices, greet, 0)
    pl.semaphore_wait(barrier, devices - 1)

    def send_head(head, carry):
        def to_peer(offset, inner):
            peer = lax.rem(me + offset, devices)
            for which, (source, target) in enumerate(((q_hbm, q_in), (k_hbm, k_in), (v_hbm, v_in))):
                pltpu.make_async_remote_copy(
                    src_ref=source.at[:, columns_of(peer * heads_here + head)],
                    dst_ref=target.at[head, rows_of(me)],
                    send_sem=qkv_send.at[which],
                    recv_sem=qkv_recv.at[which, head],
                    device_id={"ctx": peer},
                    device_id_type=MESH,
                ).start()
            return inner

        lax.fori_loop(1, devices, to_peer, 0)
        for which, (source, target) in enumerate(((q_hbm, q_in), (k_hbm, k_in), (v_hbm, v_in))):
            pltpu.make_async_copy(
                source.at[:, columns_of(me * heads_here + head)],
                target.at[head, rows_of(me)],
                qkv_recv.at[which, head],
            ).start()
        return carry

    send_head(0, 0)

    pltpu.make_async_copy(store_k, store_k, mem_load.at[0]).wait()
    pltpu.make_async_copy(store_v, store_v, mem_load.at[1]).wait()

    def pieces_of(device):
        return pl.ds(pl.multiple_of(device * pieces, pieces), pieces)

    def pack(device):
        for slot in range(capacity):
            code = send_table[device * capacity + slot]
            packed[device * pieces + 2 * slot] = store_k[code]
            packed[device * pieces + 2 * slot + 1] = store_v[code]

    def send_memory(peer):
        pltpu.make_async_remote_copy(
            src_ref=packed.at[pieces_of(peer)],
            dst_ref=arrived.at[pieces_of(me)],
            send_sem=mem_send,
            recv_sem=mem_recv,
            device_id={"ctx": peer},
            device_id_type=MESH,
        ).start()

    def pack_and_send(offset, carry):
        pack(lax.rem(me + offset + 1, devices))
        send_memory(lax.rem(me + offset, devices))
        return carry

    pack(lax.rem(me + 1, devices))
    lax.fori_loop(1, devices, pack_and_send, 0)
    pltpu.make_async_copy(packed.at[pieces_of(me)], arrived.at[pieces_of(me)], mem_recv).start()

    lax.fori_loop(1, heads_here, send_head, 0)

    def send_output(head, chunk):
        for part in range(peers_per_chunk):
            peer = chunk * peers_per_chunk + part
            source = out_buf.at[head, rows_of(peer)]
            target = out_hbm.at[:, columns_of(me * heads_here + head)]

            @pl.when(peer != me)
            def _():
                pltpu.make_async_remote_copy(
                    src_ref=source,
                    dst_ref=target,
                    send_sem=out_send,
                    recv_sem=out_recv,
                    device_id={"ctx": peer},
                    device_id_type=MESH,
                ).start()

            @pl.when(peer == me)
            def _():
                pltpu.make_async_copy(source, target, out_recv).start()

    pltpu.make_async_copy(arrived, arrived, mem_recv).wait()

    def absorb(queries, block_keys, block_values, state, masked):
        running_max, weight_sum, numerator = state
        scores = lax.dot_general(
            queries, block_keys, (((1,), (1,)), ((), ())), preferred_element_type=jnp.float32
        )
        if masked:
            row = lax.broadcasted_iota(jnp.int32, scores.shape, 0)
            column = lax.broadcasted_iota(jnp.int32, scores.shape, 1)
            scores = jnp.where(row >= column, scores, -jnp.inf)
        new_max = jnp.maximum(running_max, jnp.max(scores, axis=1, keepdims=True))
        rescale = jnp.exp2((running_max - new_max) * exponent_scale)
        weights = jnp.exp2((scores - new_max) * exponent_scale)
        weight_sum = weight_sum * rescale + jnp.sum(weights, axis=1, keepdims=True)
        numerator = numerator * rescale + jnp.dot(
            weights.astype(jnp.bfloat16), block_values, preferred_element_type=jnp.float32
        )
        return new_max, weight_sum, numerator

    def one_head(head, carry):
        for which, target in enumerate((q_in, k_in, v_in)):
            pltpu.make_async_copy(
                target.at[head], target.at[head], qkv_recv.at[which, head]
            ).wait()

        def one_chunk(chunk, inner):
            chunk_rows = pl.ds(pl.multiple_of(chunk * CHUNK, CHUNK), CHUNK)
            queries = q_in[head, chunk_rows]
            tile = chunk * CHUNK // tile_rows
            state = (
                jnp.full((CHUNK, 1), -jnp.inf, jnp.float32),
                jnp.zeros((CHUNK, 1), jnp.float32),
                jnp.zeros((CHUNK, HD), jnp.float32),
            )
            state = absorb(queries, k_in[head, chunk_rows], v_in[head, chunk_rows], state, True)
            for slot in range(listed):
                piece = receive_table[(head * tile_count + tile) * listed + slot] * 2
                state = absorb(queries, arrived[piece], arrived[piece + 1], state, False)

            def earlier(block, current):
                block_at = pl.ds(pl.multiple_of(block * CHUNK, CHUNK), CHUNK)
                return absorb(queries, k_in[head, block_at], v_in[head, block_at], current, False)

            _, weight_sum, numerator = lax.fori_loop(0, chunk, earlier, state)
            out_buf[head, chunk_rows] = (numerator / weight_sum).astype(jnp.bfloat16)

            @pl.when(chunk > 0)
            def _():
                send_output(head, chunk - 1)

            @pl.when((chunk == 0) & (head > 0))
            def _():
                send_output(head - 1, chunks - 1)

            return inner

        lax.fori_loop(0, chunks, one_chunk, 0)
        return carry

    lax.fori_loop(0, heads_here, one_head, 0)

    others = pl.ds(0, (devices - 1) * rows)
    for which, target in enumerate((q_in, k_in, v_in)):
        sent = target.at[:, others]
        pltpu.make_async_copy(sent, sent, qkv_send.at[which]).wait()
    sent = packed.at[pl.ds(0, (devices - 1) * pieces)]
    pltpu.make_async_copy(sent, sent, mem_send).wait()
    send_output(heads_here - 1, chunks - 1)
    sent = out_buf.at[:, others]
    pltpu.make_async_copy(sent, sent, out_send).wait()
    pltpu.make_async_copy(out_hbm, out_hbm, out_recv).wait()


def shards(queries, keys, values, mem_keys, mem_values, mem_ids):
    devices = lax.axis_size("ctx")
    device_index = lax.axis_index("ctx")
    head_count, tile_count, listed = mem_ids.shape
    heads_here = head_count // devices
    blocks_here, block_rows, columns = mem_keys.shape
    rows = queries.shape[0]
    span = rows * devices
    capacity = max(2, 2 * heads_here * tile_count * listed // devices)
    send_table, receive_table = entry_tables(
        mem_ids, devices, device_index, blocks_here, capacity
    )
    store = pltpu.VMEM((head_count * blocks_here, block_rows, HD), jnp.bfloat16)
    exchange = pltpu.VMEM((devices * capacity * 2, block_rows, HD), jnp.bfloat16)
    head_rows = pltpu.VMEM((heads_here, span, HD), jnp.bfloat16)
    anywhere = pl.BlockSpec(memory_space=pl.ANY)
    table = pl.BlockSpec(memory_space=pltpu.SMEM)
    return pl.pallas_call(
        functools.partial(kernel, devices, capacity, tile_count, listed),
        out_shape=jax.ShapeDtypeStruct((rows, columns), jnp.bfloat16),
        in_specs=[table, table] + [anywhere] * 5,
        out_specs=anywhere,
        scratch_shapes=[
            head_rows, head_rows, head_rows, store, store, exchange, exchange, head_rows,
            pltpu.SemaphoreType.DMA((3, heads_here)),
            pltpu.SemaphoreType.DMA((3,)),
            pltpu.SemaphoreType.DMA((2,)),
            pltpu.SemaphoreType.DMA,
            pltpu.SemaphoreType.DMA,
            pltpu.SemaphoreType.DMA,
            pltpu.SemaphoreType.DMA,
        ],
        compiler_params=pltpu.CompilerParams(
            collective_id=0, has_side_effects=True, vmem_limit_bytes=64_000_000
        ),
        name="exchange_attention",
    )(send_table, receive_table, queries, keys, values, mem_keys, mem_values)


def solution(mesh):
    in_specs = (
        P(("dp", "ctx"), None),
        P(("dp", "ctx"), None),
        P(("dp", "ctx"), None),
        P(("dp", "ctx"), None, None),
        P(("dp", "ctx"), None, None),
        P("dp", None, None),
    )
    out_specs = P(("dp", "ctx"), None)
    return jax.shard_map(shards, mesh=mesh, in_specs=in_specs, out_specs=out_specs, check_vma=False)
```

```python
import functools
import math

import jax
import jax.numpy as jnp
from jax import lax
from jax.experimental import pallas as pl
from jax.experimental.pallas import tpu as pltpu
from jax.sharding import PartitionSpec as P

HD = 128
CHUNK = 512
MESH = pl.DeviceIdType.MESH


def kernel(
    devices, capacity,
    ids, q_hbm, k_hbm, v_hbm, mk_hbm, mv_hbm, out_hbm,
    q_in, k_in, v_in, store_k, store_v, packed, arrived, out_buf,
    qkv_recv, qkv_send, mem_load, mem_recv, mem_send, out_recv, out_send,
):
    me = lax.axis_index("ctx")
    tile_count, listed, _ = ids.shape
    heads_here, span, _ = q_in.shape
    rows = q_hbm.shape[0]
    blocks_here, block_rows, columns = mk_hbm.shape
    head_count = columns // HD
    tile_rows = span // tile_count
    chunks = span // CHUNK
    peers_per_chunk = CHUNK // rows
    pieces = capacity * 2
    per_head = tile_count * listed
    entries = heads_here * per_head
    exponent_scale = HD ** (-0.5) * math.log2(math.e)

    def columns_of(head):
        return pl.ds(pl.multiple_of(head * HD, HD), HD)

    def rows_of(device):
        return pl.ds(pl.multiple_of(device * rows, rows), rows)

    def load_head(head, carry):
        for source, target, which in ((mk_hbm, store_k, 0), (mv_hbm, store_v, 1)):
            pltpu.make_async_copy(
                source.at[:, :, columns_of(head)],
                target.at[pl.ds(head * blocks_here, blocks_here)],
                mem_load.at[which],
            ).start()
        return carry

    lax.fori_loop(0, head_count, load_head, 0)

    barrier = pltpu.get_barrier_semaphore()

    def greet(offset, carry):
        pl.semaphore_signal(
            barrier, inc=1, device_id={"ctx": lax.rem(me + offset, devices)}, device_id_type=MESH
        )
        return carry

    lax.fori_loop(1, devices, greet, 0)
    pl.semaphore_wait(barrier, devices - 1)

    def send_head(head, carry):
        def to_peer(offset, inner):
            peer = lax.rem(me + offset, devices)
            for which, (source, target) in enumerate(((q_hbm, q_in), (k_hbm, k_in), (v_hbm, v_in))):
                pltpu.make_async_remote_copy(
                    src_ref=source.at[:, columns_of(peer * heads_here + head)],
                    dst_ref=target.at[head, rows_of(me)],
                    send_sem=qkv_send.at[which],
                    recv_sem=qkv_recv.at[which, head],
                    device_id={"ctx": peer},
                    device_id_type=MESH,
                ).start()
            return inner

        lax.fori_loop(1, devices, to_peer, 0)
        for which, (source, target) in enumerate(((q_hbm, q_in), (k_hbm, k_in), (v_hbm, v_in))):
            pltpu.make_async_copy(
                source.at[:, columns_of(me * heads_here + head)],
                target.at[head, rows_of(me)],
                qkv_recv.at[which, head],
            ).start()
        return carry

    send_head(0, 0)

    pltpu.make_async_copy(store_k, store_k, mem_load.at[0]).wait()
    pltpu.make_async_copy(store_v, store_v, mem_load.at[1]).wait()

    def pieces_of(device):
        return pl.ds(pl.multiple_of(device * pieces, pieces), pieces)

    def listed_block(group, entry):
        head = group * heads_here + lax.div(entry, per_head)
        return head, ids[lax.div(lax.rem(entry, per_head), listed), lax.rem(entry, listed), head]

    def pack(device):
        def look(entry, found):
            count, codes = found
            head, block = listed_block(device, entry)
            mine = lax.div(block, blocks_here) == me
            code = head * blocks_here + lax.rem(block, blocks_here)
            codes = tuple(
                jnp.where(mine & (count == slot), code, held) for slot, held in enumerate(codes)
            )
            return count + jnp.where(mine, 1, 0), codes

        zero = jnp.int32(0)
        _, codes = lax.fori_loop(0, entries, look, (zero, (zero,) * capacity))
        for slot, code in enumerate(codes):
            packed[device * pieces + 2 * slot] = store_k[code]
            packed[device * pieces + 2 * slot + 1] = store_v[code]

    def piece_of(entry):
        holder = lax.div(listed_block(me, entry)[1], blocks_here)

        def look(other, rank):
            same = lax.div(listed_block(me, other)[1], blocks_here) == holder
            return rank + jnp.where(same, 1, 0)

        return (holder * capacity + lax.fori_loop(0, entry, look, jnp.int32(0))) * 2

    def send_memory(peer):
        pltpu.make_async_remote_copy(
            src_ref=packed.at[pieces_of(peer)],
            dst_ref=arrived.at[pieces_of(me)],
            send_sem=mem_send,
            recv_sem=mem_recv,
            device_id={"ctx": peer},
            device_id_type=MESH,
        ).start()

    def pack_and_send(offset, carry):
        pack(lax.rem(me + offset + 1, devices))
        send_memory(lax.rem(me + offset, devices))
        return carry

    pack(lax.rem(me + 1, devices))
    lax.fori_loop(1, devices, pack_and_send, 0)
    pltpu.make_async_copy(packed.at[pieces_of(me)], arrived.at[pieces_of(me)], mem_recv).start()

    lax.fori_loop(1, heads_here, send_head, 0)

    def send_output(head, chunk):
        for part in range(peers_per_chunk):
            peer = chunk * peers_per_chunk + part
            source = out_buf.at[head, rows_of(peer)]
            target = out_hbm.at[:, columns_of(me * heads_here + head)]

            @pl.when(peer != me)
            def _():
                pltpu.make_async_remote_copy(
                    src_ref=source,
                    dst_ref=target,
                    send_sem=out_send,
                    recv_sem=out_recv,
                    device_id={"ctx": peer},
                    device_id_type=MESH,
                ).start()

            @pl.when(peer == me)
            def _():
                pltpu.make_async_copy(source, target, out_recv).start()

    pltpu.make_async_copy(arrived, arrived, mem_recv).wait()

    def absorb(queries, block_keys, block_values, state, masked):
        running_max, weight_sum, numerator = state
        scores = lax.dot_general(
            queries, block_keys, (((1,), (1,)), ((), ())), preferred_element_type=jnp.float32
        )
        if masked:
            row = lax.broadcasted_iota(jnp.int32, scores.shape, 0)
            column = lax.broadcasted_iota(jnp.int32, scores.shape, 1)
            scores = jnp.where(row >= column, scores, -jnp.inf)
        new_max = jnp.maximum(running_max, jnp.max(scores, axis=1, keepdims=True))
        rescale = jnp.exp2((running_max - new_max) * exponent_scale)
        weights = jnp.exp2((scores - new_max) * exponent_scale)
        weight_sum = weight_sum * rescale + jnp.sum(weights, axis=1, keepdims=True)
        numerator = numerator * rescale + jnp.dot(
            weights.astype(jnp.bfloat16), block_values, preferred_element_type=jnp.float32
        )
        return new_max, weight_sum, numerator

    def one_head(head, carry):
        for which, target in enumerate((q_in, k_in, v_in)):
            pltpu.make_async_copy(
                target.at[head], target.at[head], qkv_recv.at[which, head]
            ).wait()

        def one_chunk(step, inner):
            chunk = step
            chunk_rows = pl.ds(pl.multiple_of(chunk * CHUNK, CHUNK), CHUNK)
            queries = q_in[head, chunk_rows]
            tile = lax.div(chunk * CHUNK, tile_rows)
            state = (
                jnp.full((CHUNK, 1), -jnp.inf, jnp.float32),
                jnp.zeros((CHUNK, 1), jnp.float32),
                jnp.zeros((CHUNK, HD), jnp.float32),
            )
            state = absorb(queries, k_in[head, chunk_rows], v_in[head, chunk_rows], state, True)
            for slot in range(listed):
                piece = piece_of((head * tile_count + tile) * listed + slot)
                state = absorb(queries, arrived[piece], arrived[piece + 1], state, False)

            def earlier(block, current):
                block_at = pl.ds(pl.multiple_of(block * CHUNK, CHUNK), CHUNK)
                return absorb(queries, k_in[head, block_at], v_in[head, block_at], current, False)

            _, weight_sum, numerator = lax.fori_loop(0, chunk, earlier, state)
            out_buf[head, chunk_rows] = (numerator / weight_sum).astype(jnp.bfloat16)

            @pl.when(step > 0)
            def _():
                send_output(head, step - 1)

            @pl.when((step == 0) & (head > 0))
            def _():
                send_output(head - 1, chunks - 1)

            return inner

        lax.fori_loop(0, chunks, one_chunk, 0)
        return carry

    lax.fori_loop(0, heads_here, one_head, 0)

    others = pl.ds(0, (devices - 1) * rows)
    for which, target in enumerate((q_in, k_in, v_in)):
        sent = target.at[:, others]
        pltpu.make_async_copy(sent, sent, qkv_send.at[which]).wait()
    sent = packed.at[pl.ds(0, (devices - 1) * pieces)]
    pltpu.make_async_copy(sent, sent, mem_send).wait()
    send_output(heads_here - 1, chunks - 1)
    sent = out_buf.at[:, others]
    pltpu.make_async_copy(sent, sent, out_send).wait()
    pltpu.make_async_copy(out_hbm, out_hbm, out_recv).wait()


def hand_over(source_ref, target_ref):
    target_ref[...] = source_ref[...]


def shards(queries, keys, values, mem_keys, mem_values, mem_ids):
    devices = lax.axis_size("ctx")
    head_count, tile_count, listed = mem_ids.shape
    heads_here = head_count // devices
    blocks_here, block_rows, columns = mem_keys.shape
    rows = queries.shape[0]
    span = rows * devices
    capacity = max(2, 2 * heads_here * tile_count * listed // devices)
    store = pltpu.VMEM((head_count * blocks_here, block_rows, HD), jnp.bfloat16)
    exchange = pltpu.VMEM((devices * capacity * 2, block_rows, HD), jnp.bfloat16)
    head_rows = pltpu.VMEM((heads_here, span, HD), jnp.bfloat16)
    anywhere = pl.BlockSpec(memory_space=pl.ANY)
    table = pl.BlockSpec(memory_space=pltpu.SMEM)
    attended = pl.pallas_call(
        functools.partial(kernel, devices, capacity),
        out_shape=jax.ShapeDtypeStruct((rows, columns), jnp.bfloat16),
        in_specs=[table] + [anywhere] * 5,
        out_specs=anywhere,
        scratch_shapes=[
            head_rows, head_rows, head_rows, store, store, exchange, exchange, head_rows,
            pltpu.SemaphoreType.DMA((3, heads_here)),
            pltpu.SemaphoreType.DMA((3,)),
            pltpu.SemaphoreType.DMA((2,)),
            pltpu.SemaphoreType.DMA,
            pltpu.SemaphoreType.DMA,
            pltpu.SemaphoreType.DMA,
            pltpu.SemaphoreType.DMA,
        ],
        compiler_params=pltpu.CompilerParams(
            collective_id=0, has_side_effects=True, vmem_limit_bytes=64_000_000
        ),
        name="exchange_attention",
    )(mem_ids.transpose(1, 2, 0), queries, keys, values, mem_keys, mem_values)
    block = pl.BlockSpec((rows // 4, columns), lambda step: (step, 0))
    return pl.pallas_call(
        hand_over,
        out_shape=jax.ShapeDtypeStruct((rows, columns), jnp.bfloat16),
        grid=(4,),
        in_specs=[block],
        out_specs=block,
        name="hand_over",
    )(attended)


def solution(mesh):
    in_specs = (
        P(("dp", "ctx"), None),
        P(("dp", "ctx"), None),
        P(("dp", "ctx"), None),
        P(("dp", "ctx"), None, None),
        P(("dp", "ctx"), None, None),
        P("dp", None, None),
    )
    out_specs = P(("dp", "ctx"), None)
    return jax.shard_map(shards, mesh=mesh, in_specs=in_specs, out_specs=out_specs, check_vma=False)
```

```python
import functools
import math

import jax
import jax.numpy as jnp
from jax import lax
from jax.experimental import pallas as pl
from jax.experimental.pallas import tpu as pltpu
from jax.sharding import PartitionSpec as P

HD = 128
CHUNK = 512
MESH = pl.DeviceIdType.MESH


def kernel(
    devices, capacity,
    ids, q_hbm, k_hbm, v_hbm, mk_hbm, mv_hbm, out_hbm,
    q_in, k_in, v_in, store_k, store_v, packed, arrived, out_buf,
    qkv_recv, qkv_send, mem_load, mem_recv, mem_send, out_recv, out_send,
):
    me = lax.axis_index("ctx")
    tile_count, listed, _ = ids.shape
    heads_here, span, _ = q_in.shape
    rows = q_hbm.shape[0]
    blocks_here, block_rows, columns = mk_hbm.shape
    head_count = columns // HD
    tile_rows = span // tile_count
    chunks = span // CHUNK
    peers_per_chunk = CHUNK // rows
    pieces = capacity * 2
    per_head = tile_count * listed
    entries = heads_here * per_head
    exponent_scale = HD ** (-0.5) * math.log2(math.e)

    def columns_of(head):
        return pl.ds(pl.multiple_of(head * HD, HD), HD)

    def rows_of(device):
        return pl.ds(pl.multiple_of(device * rows, rows), rows)

    def load_head(head, carry):
        for source, target, which in ((mk_hbm, store_k, 0), (mv_hbm, store_v, 1)):
            pltpu.make_async_copy(
                source.at[:, :, columns_of(head)],
                target.at[pl.ds(head * blocks_here, blocks_here)],
                mem_load.at[which],
            ).start()
        return carry

    lax.fori_loop(0, head_count, load_head, 0)

    barrier = pltpu.get_barrier_semaphore()

    def greet(offset, carry):
        pl.semaphore_signal(
            barrier, inc=1, device_id={"ctx": lax.rem(me + offset, devices)}, device_id_type=MESH
        )
        return carry

    lax.fori_loop(1, devices, greet, 0)
    pl.semaphore_wait(barrier, devices - 1)

    def send_head(head, carry):
        def to_peer(offset, inner):
            peer = lax.rem(me + offset, devices)
            for which, (source, target) in enumerate(((q_hbm, q_in), (k_hbm, k_in), (v_hbm, v_in))):
                pltpu.make_async_remote_copy(
                    src_ref=source.at[:, columns_of(peer * heads_here + head)],
                    dst_ref=target.at[head, rows_of(me)],
                    send_sem=qkv_send.at[which],
                    recv_sem=qkv_recv.at[which, head],
                    device_id={"ctx": peer},
                    device_id_type=MESH,
                ).start()
            return inner

        lax.fori_loop(1, devices, to_peer, 0)
        for which, (source, target) in enumerate(((q_hbm, q_in), (k_hbm, k_in), (v_hbm, v_in))):
            pltpu.make_async_copy(
                source.at[:, columns_of(me * heads_here + head)],
                target.at[head, rows_of(me)],
                qkv_recv.at[which, head],
            ).start()
        return carry

    send_head(0, 0)

    pltpu.make_async_copy(store_k, store_k, mem_load.at[0]).wait()
    pltpu.make_async_copy(store_v, store_v, mem_load.at[1]).wait()

    def pieces_of(device):
        return pl.ds(pl.multiple_of(device * pieces, pieces), pieces)

    def listed_block(group, entry):
        head = group * heads_here + lax.div(entry, per_head)
        return head, ids[lax.div(lax.rem(entry, per_head), listed), lax.rem(entry, listed), head]

    def pack(device):
        def look(entry, found):
            count, codes = found
            head, block = listed_block(device, entry)
            mine = lax.div(block, blocks_here) == me
            code = head * blocks_here + lax.rem(block, blocks_here)
            codes = tuple(
                jnp.where(mine & (count == slot), code, held) for slot, held in enumerate(codes)
            )
            return count + jnp.where(mine, 1, 0), codes

        zero = jnp.int32(0)
        _, codes = lax.fori_loop(0, entries, look, (zero, (zero,) * capacity))
        for slot, code in enumerate(codes):
            packed[device * pieces + 2 * slot] = store_k[code]
            packed[device * pieces + 2 * slot + 1] = store_v[code]

    def piece_of(entry):
        holder = lax.div(listed_block(me, entry)[1], blocks_here)

        def look(other, rank):
            same = lax.div(listed_block(me, other)[1], blocks_here) == holder
            return rank + jnp.where(same, 1, 0)

        return (holder * capacity + lax.fori_loop(0, entry, look, jnp.int32(0))) * 2

    def send_memory(peer):
        pltpu.make_async_remote_copy(
            src_ref=packed.at[pieces_of(peer)],
            dst_ref=arrived.at[pieces_of(me)],
            send_sem=mem_send,
            recv_sem=mem_recv,
            device_id={"ctx": peer},
            device_id_type=MESH,
        ).start()

    def pack_and_send(offset, carry):
        pack(lax.rem(me + offset + 1, devices))
        send_memory(lax.rem(me + offset, devices))
        return carry

    pack(lax.rem(me + 1, devices))
    lax.fori_loop(1, devices, pack_and_send, 0)
    pltpu.make_async_copy(packed.at[pieces_of(me)], arrived.at[pieces_of(me)], mem_recv).start()

    lax.fori_loop(1, heads_here, send_head, 0)

    def send_output(head, chunk):
        for part in range(peers_per_chunk):
            peer = chunk * peers_per_chunk + part
            source = out_buf.at[head, rows_of(peer)]
            target = out_hbm.at[:, columns_of(me * heads_here + head)]

            @pl.when(peer != me)
            def _():
                pltpu.make_async_remote_copy(
                    src_ref=source,
                    dst_ref=target,
                    send_sem=out_send,
                    recv_sem=out_recv,
                    device_id={"ctx": peer},
                    device_id_type=MESH,
                ).start()

            @pl.when(peer == me)
            def _():
                pltpu.make_async_copy(source, target, out_recv).start()

    pltpu.make_async_copy(arrived, arrived, mem_recv).wait()

    def absorb(queries, block_keys, block_values, state, masked):
        running_max, weight_sum, numerator = state
        scores = lax.dot_general(
            queries, block_keys, (((1,), (1,)), ((), ())), preferred_element_type=jnp.float32
        )
        if masked:
            row = lax.broadcasted_iota(jnp.int32, scores.shape, 0)
            column = lax.broadcasted_iota(jnp.int32, scores.shape, 1)
            scores = jnp.where(row >= column, scores, -jnp.inf)
        new_max = jnp.maximum(running_max, jnp.max(scores, axis=1, keepdims=True))
        rescale = jnp.exp2((running_max - new_max) * exponent_scale)
        weights = jnp.exp2((scores - new_max) * exponent_scale)
        weight_sum = weight_sum * rescale + jnp.sum(weights, axis=1, keepdims=True)
        numerator = numerator * rescale + jnp.dot(
            weights.astype(jnp.bfloat16), block_values, preferred_element_type=jnp.float32
        )
        return new_max, weight_sum, numerator

    def one_head(head, carry):
        for which, target in enumerate((q_in, k_in, v_in)):
            pltpu.make_async_copy(
                target.at[head], target.at[head], qkv_recv.at[which, head]
            ).wait()

        def one_chunk(step, inner):
            chunk = step
            chunk_rows = pl.ds(pl.multiple_of(chunk * CHUNK, CHUNK), CHUNK)
            queries = q_in[head, chunk_rows]
            tile = lax.div(chunk * CHUNK, tile_rows)
            state = (
                jnp.full((CHUNK, 1), -jnp.inf, jnp.float32),
                jnp.zeros((CHUNK, 1), jnp.float32),
                jnp.zeros((CHUNK, HD), jnp.float32),
            )
            state = absorb(queries, k_in[head, chunk_rows], v_in[head, chunk_rows], state, True)
            for slot in range(listed):
                piece = piece_of((head * tile_count + tile) * listed + slot)
                state = absorb(queries, arrived[piece], arrived[piece + 1], state, False)

            def earlier(block, current):
                block_at = pl.ds(pl.multiple_of(block * CHUNK, CHUNK), CHUNK)
                return absorb(queries, k_in[head, block_at], v_in[head, block_at], current, False)

            _, weight_sum, numerator = lax.fori_loop(0, chunk, earlier, state)
            out_buf[head, chunk_rows] = (numerator / weight_sum).astype(jnp.bfloat16)

            @pl.when(step > 0)
            def _():
                send_output(head, step - 1)

            @pl.when((step == 0) & (head > 0))
            def _():
                send_output(head - 1, chunks - 1)

            return inner

        lax.fori_loop(0, chunks, one_chunk, 0)
        return carry

    lax.fori_loop(0, heads_here, one_head, 0)

    others = pl.ds(0, (devices - 1) * rows)
    for which, target in enumerate((q_in, k_in, v_in)):
        sent = target.at[:, others]
        pltpu.make_async_copy(sent, sent, qkv_send.at[which]).wait()
    sent = packed.at[pl.ds(0, (devices - 1) * pieces)]
    pltpu.make_async_copy(sent, sent, mem_send).wait()
    send_output(heads_here - 1, chunks - 1)
    sent = out_buf.at[:, others]
    pltpu.make_async_copy(sent, sent, out_send).wait()
    pltpu.make_async_copy(out_hbm, out_hbm, out_recv).wait()


def shards(queries, keys, values, mem_keys, mem_values, mem_ids):
    devices = lax.axis_size("ctx")
    head_count, tile_count, listed = mem_ids.shape
    heads_here = head_count // devices
    blocks_here, block_rows, columns = mem_keys.shape
    rows = queries.shape[0]
    span = rows * devices
    capacity = max(2, 2 * heads_here * tile_count * listed // devices)
    store = pltpu.VMEM((head_count * blocks_here, block_rows, HD), jnp.bfloat16)
    exchange = pltpu.VMEM((devices * capacity * 2, block_rows, HD), jnp.bfloat16)
    head_rows = pltpu.VMEM((heads_here, span, HD), jnp.bfloat16)
    anywhere = pl.BlockSpec(memory_space=pl.ANY)
    table = pl.BlockSpec(memory_space=pltpu.SMEM)
    return pl.pallas_call(
        functools.partial(kernel, devices, capacity),
        out_shape=pltpu.VMEM((rows, columns), jnp.bfloat16),
        in_specs=[table] + [anywhere] * 5,
        out_specs=pl.BlockSpec(memory_space=pltpu.VMEM),
        scratch_shapes=[
            head_rows, head_rows, head_rows, store, store, exchange, exchange, head_rows,
            pltpu.SemaphoreType.DMA((3, heads_here)),
            pltpu.SemaphoreType.DMA((3,)),
            pltpu.SemaphoreType.DMA((2,)),
            pltpu.SemaphoreType.DMA,
            pltpu.SemaphoreType.DMA,
            pltpu.SemaphoreType.DMA,
            pltpu.SemaphoreType.DMA,
        ],
        compiler_params=pltpu.CompilerParams(
            collective_id=0, has_side_effects=True, vmem_limit_bytes=60_000_000
        ),
        name="exchange_attention",
    )(mem_ids.transpose(1, 2, 0), queries, keys, values, mem_keys, mem_values)


def solution(mesh):
    in_specs = (
        P(("dp", "ctx"), None),
        P(("dp", "ctx"), None),
        P(("dp", "ctx"), None),
        P(("dp", "ctx"), None, None),
        P(("dp", "ctx"), None, None),
        P("dp", None, None),
    )
    out_specs = P(("dp", "ctx"), None)
    return jax.shard_map(shards, mesh=mesh, in_specs=in_specs, out_specs=out_specs, check_vma=False)
```
